32 devices in a mesh: run: 1, row: 16 (over z, y, core), col: 1, seg: 2 (over x).
Axes of the slice: x: 2, y: 2, z: 4, core: 2. Of those that a mesh axis runs over, the one named last changes fastest.
Arguments:
- traces: bfloat16 [2, 1024, 2048], P(('run', 'seg'), 'row', 'col'), may hold values from -30 to 30
- live_mask: int32 [1024], P(('run', 'row')), may hold values 0 or 1
- sources: int32 [64], replicated, may hold values from 0 to 1023
- owners: int32 [64, 1], replicated, may hold values from 0 to 15; in each aligned block of 64 rows (0 to 63, 64 to 127, ...) at most 12 rows name the same one
Outputs:
- gathers: bfloat16 [192, 16, 64, 256], P(('run', 'row'), None, ('col', 'seg'))
The draws below stay inside these ranges and needn't reach their ends.
Inputs may be any that keep to these rules, and one draw needn't show every extreme that they name: `owners`: at most 12 sources share an owner, and some owner has exactly 12.
All inputs are finite; a program needn't handle non-finite values. No bound on the sum of `live_mask` on one device may be relied on, other than what follows from the above.
Results may differ from the reference program's by a relative error of at most 0.024.
Values may be sent and summed in bfloat16 or wider, within the bound.
No kernel may reach another device: no remote copies, remote signals or barrier semaphores. Data moves between devices by JAX's collectives and lax.ppermute only.
A program may use at most 64 MiB of HBM per device.

```python
import math
import jax
import jax.numpy as jnp
import numpy as np
from jax import lax

NT = 2048
NF = 1024
LAGS = 256
BAND = 64
CB = 64
V = 64
NSEG = 2
CH = 1024
CAP = 12
N_ROW = 16
N_COL = 1


def draw_traces(key, part):
    keys = jax.random.split(jax.random.fold_in(key, 7), 5)
    shape = (NSEG, CH, NT)
    noise = jnp.clip(jax.random.normal(keys[0], shape, jnp.float32), -5.0, 5.0)
    amplitude = jnp.exp(jax.random.uniform(keys[1], (NSEG, CH, 1), jnp.float32, math.log(0.3), math.log(3.0)))
    tone_bins = jax.random.randint(keys[2], (1, CH, 1), 1, NF)
    tone_size = jnp.exp(jax.random.uniform(keys[3], (1, CH, 1), jnp.float32, math.log(0.2), math.log(1.0)))
    tone_phase = jax.random.uniform(keys[4], (1, CH, 1), jnp.float32, -math.pi, math.pi)
    sample_ids = jnp.arange(NT, dtype=jnp.int32)[None, None, :]
    angles = (tone_bins * sample_ids % NT).astype(jnp.float32) * (2.0 * math.pi / NT) + tone_phase
    return (amplitude * (noise + tone_size * jnp.cos(angles))).astype(jnp.bfloat16)


def place_ends(drawn, stream_key, smallest, high):
    index_at = [jax.random.randint(jax.random.fold_in(stream_key, axis), (), 0, length) for axis, length in enumerate(drawn.shape)]
    widest = drawn.shape.index(max(drawn.shape))
    beside = index_at[:widest] + [(index_at[widest] + 1) % drawn.shape[widest]] + index_at[widest + 1:]
    return drawn.at[tuple(index_at)].set(smallest).at[tuple(beside)].set(high)


def deal_out(key, own, number, rows, number_of, top, reach, lean):
    order = jax.random.permutation(key, number_of)
    crowded, ordinary = shares(number_of, rows * top, reach, lean, True), shares(number_of, rows * top, reach, lean, False)
    places = jnp.arange(number_of)

    def named(sizes, offset_by):
        used = int((sizes > 0).sum())
        fixed = max(1, used // 4)
        moved = fixed + (places - fixed + offset_by * (used - fixed)) % max(1, number_of - fixed)
        return jnp.zeros((number_of,), jnp.int32).at[order[jnp.where(places < fixed, places, moved)]].set(jnp.asarray(sizes, jnp.int32))

    sizes = jnp.where(number % 4 == 0, named(crowded, number // 4), named(ordinary, number - number // 4 - 1))
    mixed = jax.random.permutation(jax.random.fold_in(own, 3), number_of)
    source_of, sink = mixed[0:number_of // 2 * 2:2], mixed[1:number_of // 2 * 2:2]
    room = jnp.minimum(sizes[source_of] - 1, reach - sizes[sink]) // 2
    room = jnp.where((source_of == order[0]) | (sink == order[0]) | (sizes[sink] == 0), 0, jnp.maximum(room, 0))
    moved = jax.random.randint(jax.random.fold_in(own, 4), (number_of // 2,), 0, 1 << 20) % (room + 1)
    sizes = sizes.at[source_of].add(-moved).at[sink].add(moved)
    labels = jnp.searchsorted(jnp.cumsum(sizes), jnp.arange(rows * top), side="right").astype(jnp.int32)
    table = labels.reshape(top, rows).T
    table = table[jax.random.permutation(jax.random.fold_in(own, 1), rows)]
    offset_by = jax.random.randint(jax.random.fold_in(own, 2), (rows, 1), 0, top)
    return jnp.take_along_axis(table, (jnp.arange(top)[None, :] + offset_by) % top, axis=1)


def shares(amount, total, bound, skew, full):
    weights = [(1 << 20) // math.isqrt(standing ** skew) + 1 for standing in range(1, amount + 1)]
    largest = bound if full else min(bound, max(-(-total // amount), total * weights[0] // sum(weights)))
    least = 1 if total - largest >= amount - 1 else 0
    given, surplus = [largest] + [least] * (amount - 1), total - largest - least * (amount - 1)
    while surplus > 0:
        movable = [i for i in range(1, amount) if given[i] < largest] or [i for i in range(1, amount) if given[i] < bound]
        mass, remaining = sum([weights[i] for i in movable]), surplus
        for i in movable:
            extra = min(bound - given[i], max(1, remaining * weights[i] // mass), surplus)
            given[i] = given[i] + extra
            surplus = surplus - extra
    return np.array(given)


def setup_inputs(seed: int = 0, part: int = 0) -> dict:
    arg_keys = jax.random.split(jax.random.key(seed), 5)
    part_splits = jax.random.split(jax.random.fold_in(arg_keys[4], part), 5)
    traces = draw_traces(jax.random.fold_in(jax.random.fold_in(arg_keys[4], part), 71), part)
    live_mask = place_ends((jax.random.randint(part_splits[1], (CH,), 0, 16) < 15).astype(jnp.int32), jax.random.fold_in(part_splits[1], 1), 0, 1)
    sources = place_ends(jax.random.randint(arg_keys[2], (V,), 0, CH), jax.random.fold_in(arg_keys[2], 1), 0, CH - 1).astype(jnp.int32)
    owners_keys = jax.random.split(jax.random.fold_in(arg_keys[3], 1), V // V)
    owners_turns = jax.random.permutation(jax.random.fold_in(arg_keys[3], 3), V // V)
    owners = jax.vmap(lambda own, number: deal_out(jax.random.fold_in(arg_keys[3], 2), own, number, V, N_ROW, 1, CAP, 2))(owners_keys, owners_turns).reshape((V, 1))
    return {"traces": traces, "live_mask": live_mask, "sources": sources, "owners": owners}


two_pi = 2.0 * math.pi

def turn_table(first_ids, second_ids, period):
    product = first_ids[:, None] * second_ids[None, :] % period
    return product.astype(jnp.float32) * (two_pi / period)

def reference(traces, live_mask, sources, owners):
    sample_ids = jnp.arange(NT, dtype=jnp.int32)
    bin_ids = jnp.arange(NF, dtype=jnp.int32)
    angles = turn_table(sample_ids, bin_ids, NT)
    cosine = jnp.cos(angles).astype(jnp.bfloat16)
    sine_table = jnp.sin(angles).astype(jnp.bfloat16)
    flat = traces.reshape(NSEG * CH, NT)
    real_part = jnp.dot(flat, cosine, preferred_element_type=jnp.float32)
    imag_part = -jnp.dot(flat, sine_table, preferred_element_type=jnp.float32)
    band_power = (real_part * real_part + imag_part * imag_part).reshape(NSEG * CH, NF // BAND, BAND)
    band_power = lax.optimization_barrier(jnp.sum(band_power, axis=-1)) / (2 * BAND) + 1e-05
    living = jnp.tile(live_mask.astype(jnp.float32), NSEG)
    scaling = living[:, None] / jnp.sqrt(band_power)
    scaling = jnp.repeat(scaling, BAND, axis=1)
    white_real = (real_part * scaling).astype(jnp.bfloat16).reshape(NSEG, CH, NF)
    white_imag = (imag_part * scaling).astype(jnp.bfloat16).reshape(NSEG, CH, NF)
    source_real = white_real[:, sources, :]
    source_imag = white_imag[:, sources, :]
    lag_ids = jnp.arange(LAGS, dtype=jnp.int32) - LAGS // 2 + NT
    lag_angles = turn_table(bin_ids, lag_ids, NT)
    lag_cos = jnp.cos(lag_angles).astype(jnp.bfloat16)
    lag_sin = jnp.sin(lag_angles).astype(jnp.bfloat16)
    half_bins = NF // N_COL
    block_rows = min(CH, 128)

    def receiver_block(first_row):
        total = jnp.zeros((block_rows, V, LAGS), jnp.float32)
        for segment in range(NSEG):
            for half in range(N_COL):
                low = half * half_bins
                high = low + half_bins
                recv_real = lax.dynamic_slice_in_dim(white_real[segment, :, low:high], first_row, block_rows, 0).astype(jnp.float32)
                recv_imag = lax.dynamic_slice_in_dim(white_imag[segment, :, low:high], first_row, block_rows, 0).astype(jnp.float32)
                real_source = source_real[segment, :, low:high].astype(jnp.float32)
                imag_source = source_imag[segment, :, low:high].astype(jnp.float32)
                cross_real = (real_source[None, :, :] * recv_real[:, None, :] + imag_source[None, :, :] * recv_imag[:, None, :]).astype(jnp.bfloat16)
                cross_imag = (imag_source[None, :, :] * recv_real[:, None, :] - real_source[None, :, :] * recv_imag[:, None, :]).astype(jnp.bfloat16)
                table = jnp.concatenate([lag_cos[low:high], -lag_sin[low:high]], axis=0).astype(jnp.float32)
                stacked_cross = jnp.concatenate([cross_real, cross_imag], axis=2).astype(jnp.float32)
                term = jnp.einsum('gvf,fl->gvl', stacked_cross, table)
                total = total + lax.optimization_barrier(term.astype(jnp.bfloat16)).astype(jnp.float32)
        return total
    starts = jnp.arange(CH // block_rows, dtype=jnp.int32) * block_rows
    stacked = lax.map(receiver_block, starts).reshape(CH, V, LAGS)
    mean_sq = lax.optimization_barrier(jnp.mean(stacked * stacked, axis=-1, keepdims=True))
    normed = (stacked / jnp.sqrt(mean_sq + 1e-06)).astype(jnp.bfloat16)
    owner_ids = owners[:, 0]
    order_ids = jnp.arange(V, dtype=jnp.int32)
    earlier = (owner_ids[:, None] == owner_ids[None, :]) & (order_ids[None, :] < order_ids[:, None])
    slot_rank = lax.optimization_barrier(jnp.sum(earlier.astype(jnp.int32), axis=1))
    slot_ids = (owner_ids * CAP + slot_rank).astype(jnp.int32)
    gathers = jnp.zeros((N_ROW * CAP, CH, LAGS), jnp.bfloat16).at[slot_ids].set(jnp.transpose(normed, (1, 0, 2)))
    return gathers.reshape(N_ROW * CAP, N_ROW, CB, LAGS)
```

```python
import functools
import math

import jax
import jax.numpy as jnp
from jax import lax
from jax.experimental import pallas as pl
from jax.experimental.pallas import tpu as pltpu
from jax.sharding import PartitionSpec as P

NT = 2048
NF = 1024
LAGS = 256
BAND = 64


two_pi = 2.0 * math.pi
f32 = jnp.float32
bf16 = jnp.bfloat16


def turn_table(first_ids, second_ids, period):
    product = first_ids[:, None] * second_ids[None, :] % period
    return product.astype(jnp.float32) * (two_pi / period)


def lag_matrix(bin_ids):
    lag_ids = jnp.arange(LAGS, dtype=jnp.int32) - LAGS // 2 + NT
    lag_angles = turn_table(bin_ids, lag_ids, NT)
    return jnp.concatenate(
        [jnp.cos(lag_angles).astype(jnp.bfloat16), -jnp.sin(lag_angles).astype(jnp.bfloat16)],
        axis=0,
    )


def correlate(recv_real, recv_imag, real_source, imag_source, lag_table):
    cross_real = (
        real_source[:, None, :] * recv_real[:, :, None]
        + imag_source[:, None, :] * recv_imag[:, :, None]
    ).astype(jnp.bfloat16)
    cross_imag = (
        imag_source[:, None, :] * recv_real[:, :, None]
        - real_source[:, None, :] * recv_imag[:, :, None]
    ).astype(jnp.bfloat16)
    stacked_cross = jnp.concatenate([cross_real, cross_imag], axis=0)
    return jnp.einsum("fl,fgv->gvl", lag_table, stacked_cross, preferred_element_type=jnp.float32)


def local_general(traces, live_mask, sources, owners):
    col_count = lax.axis_size("col")
    seg_count = lax.axis_size("seg")
    row_count = lax.axis_size("row")
    samples = traces[0]
    channels = samples.shape[0]
    local_width = samples.shape[1]
    num_sources = sources.shape[0]
    first_sample = lax.axis_index("col") * local_width
    half_bins = NF // col_count
    sample_ids = first_sample + jnp.arange(local_width, dtype=jnp.int32)
    bin_ids = jnp.arange(half_bins * lax.axis_size("col"), dtype=jnp.int32)
    angles = turn_table(sample_ids, bin_ids, NT)
    cosine = jnp.cos(angles).astype(jnp.bfloat16)
    sine_table = jnp.sin(angles).astype(jnp.bfloat16)
    real_part = jnp.einsum("tf,ct->fc", cosine, samples, preferred_element_type=jnp.float32)
    imag_part = -jnp.einsum("tf,ct->fc", sine_table, samples, preferred_element_type=jnp.float32)
    spectra = lax.psum_scatter(
        jnp.concatenate([real_part, imag_part], axis=1).astype(jnp.bfloat16),
        "col",
        scatter_dimension=0,
        tiled=True,
    ).astype(jnp.float32)
    squares = (spectra * spectra).reshape(half_bins // BAND, BAND, 2, channels)
    band_power = jnp.sum(squares, axis=(1, 2)) / (2 * BAND) + 1e-05
    scaling = live_mask.astype(jnp.float32)[None, :] / jnp.sqrt(band_power)
    scaling = jnp.repeat(scaling, BAND, axis=0)
    whitened = (
        (spectra.reshape(half_bins, 2, channels) * scaling[:, None, :])
        .reshape(half_bins, 2 * channels)
        .astype(jnp.bfloat16)
    )
    white_real = whitened[:, :channels]
    white_imag = whitened[:, channels:]
    everyone = lax.all_gather(whitened, "row", axis=1, tiled=True)
    block_ids = sources // channels
    within = sources % channels
    real_cols = block_ids * (2 * channels) + within
    source_real = jnp.take(everyone, real_cols, axis=1)
    source_imag = jnp.take(everyone, real_cols + channels, axis=1)
    receivers = channels // (col_count * seg_count)
    bin_ids = lax.axis_index("col") * half_bins + jnp.arange(half_bins, dtype=jnp.int32)
    lag_table = lag_matrix(bin_ids)
    real_source = source_real.astype(jnp.float32)
    imag_source = source_imag.astype(jnp.float32)

    def one_group(offset):
        recv_real = lax.dynamic_slice_in_dim(white_real, offset, receivers, 1).astype(jnp.float32)
        recv_imag = lax.dynamic_slice_in_dim(white_imag, offset, receivers, 1).astype(jnp.float32)
        return correlate(recv_real, recv_imag, real_source, imag_source, lag_table)

    offsets = (
        jnp.arange(receivers * lax.axis_size(("col", "seg")) // receivers, dtype=jnp.int32)
        * receivers
    )
    blocks = lax.map(one_group, offsets)
    stacked = lax.psum_scatter(
        blocks.reshape(receivers * lax.axis_size(("col", "seg")), num_sources, LAGS).astype(
            jnp.bfloat16
        ),
        ("col", "seg"),
        scatter_dimension=0,
        tiled=True,
    ).astype(jnp.float32)
    mean_sq = jnp.mean(stacked * stacked, axis=-1, keepdims=True)
    normed = (stacked / jnp.sqrt(mean_sq + 1e-06)).astype(jnp.bfloat16)
    capacity = 3 * num_sources // row_count
    owner_ids = owners[:, 0]
    order_ids = jnp.arange(num_sources, dtype=jnp.int32)
    earlier = (owner_ids[:, None] == owner_ids[None, :]) & (order_ids[None, :] < order_ids[:, None])
    slot_rank = jnp.sum(earlier.astype(jnp.int32), axis=1)
    slot_ids = owner_ids * capacity + slot_rank
    placing = (
        jnp.arange(row_count * capacity, dtype=jnp.int32)[:, None] == slot_ids[None, :]
    ).astype(jnp.bfloat16)
    outgoing = jnp.einsum(
        "sv,gvl->sgl", placing, normed, preferred_element_type=jnp.float32
    ).astype(jnp.bfloat16)
    return lax.all_to_all(outgoing[:, None], "row", split_axis=0, concat_axis=1, tiled=True)


HALF = NT // 2
QUARTER = NF // 2
VMEM_LIMIT = 40 * 1024 * 1024


def dft_seeds():
    bins = jnp.concatenate([jnp.arange(0, NF, 2), jnp.arange(1, NF, 2)]).astype(jnp.int32)
    steps = jnp.concatenate(
        [jnp.arange(HALF // 64) * 64, jnp.arange(8) * 8, jnp.arange(8)]
    ).astype(jnp.int32)
    angles = turn_table(steps, bins, NT)
    return jnp.cos(angles), jnp.sin(angles)


def lag_seeds():
    lags = jnp.arange(LAGS, dtype=jnp.int32) - LAGS // 2 + NT
    steps = jnp.concatenate(
        [
            jnp.arange(QUARTER // 64) * 128,
            jnp.arange(8) * 16,
            jnp.arange(8) * 2,
            jnp.arange(8) * 2 + 1,
        ]
    ).astype(jnp.int32)
    angles = turn_table(steps, lags, NT)
    return jnp.cos(angles), jnp.sin(angles)


def tables_kernel(dc, ds, lc, ls, dft_ref, lag_ref, base_c, base_s):
    blocks = HALF // 64
    for b in range(8):
        cb, sb = dc[blocks + b : blocks + b + 1, :], ds[blocks + b : blocks + b + 1, :]
        cc, sc = dc[blocks + 8 : blocks + 16, :], ds[blocks + 8 : blocks + 16, :]
        base_c[8 * b : 8 * b + 8, :] = cc * cb - sc * sb
        base_s[8 * b : 8 * b + 8, :] = sc * cb + cc * sb
    for a in range(blocks):
        for lo in range(0, NF, 256):
            ca, sa = dc[a : a + 1, lo : lo + 256], ds[a : a + 1, lo : lo + 256]
            bc, bs = base_c[:, lo : lo + 256], base_s[:, lo : lo + 256]
            dft_ref[64 * a : 64 * a + 64, lo : lo + 256] = (bc * ca - bs * sa).astype(bf16)
            dft_ref[64 * a : 64 * a + 64, NF + lo : NF + lo + 256] = (-bs * ca - bc * sa).astype(bf16)
    groups = QUARTER // 64
    for odd in range(2):
        first = groups + 8 + 8 * odd
        cc, sc = lc[first : first + 8, :], ls[first : first + 8, :]
        for b in range(8):
            cb, sb = lc[groups + b : groups + b + 1, :], ls[groups + b : groups + b + 1, :]
            base_c[8 * b : 8 * b + 8, :LAGS] = cc * cb - sc * sb
            base_s[8 * b : 8 * b + 8, :LAGS] = sc * cb + cc * sb
        for a in range(groups):
            ca, sa = lc[a : a + 1, :], ls[a : a + 1, :]
            bc, bs = base_c[:, :LAGS], base_s[:, :LAGS]
            at = QUARTER * odd + 64 * a
            lag_ref[at : at + 64, :] = (bc * ca - bs * sa).astype(bf16)
            lag_ref[NF + at : NF + at + 64, :] = (-bs * ca - bc * sa).astype(bf16)


def make_tables():
    dc, ds = dft_seeds()
    lc, ls = lag_seeds()
    return pl.pallas_call(
        tables_kernel,
        out_shape=(
            jax.ShapeDtypeStruct((HALF, 2 * NF), bf16),
            jax.ShapeDtypeStruct((2 * NF, LAGS), bf16),
        ),
        scratch_shapes=[pltpu.VMEM((64, NF), f32), pltpu.VMEM((64, NF), f32)],
        compiler_params=pltpu.CompilerParams(vmem_limit_bytes=VMEM_LIMIT),
        cost_estimate=pl.CostEstimate(
            flops=6 * HALF * NF, bytes_accessed=4 * HALF * NF, transcendentals=0
        ),
        name="tables",
    )(dc, ds, lc, ls)


def whiten_kernel(own_ref, other_ref, live_ref, dft_ref, out_ref):
    rows = own_ref.shape[0]
    own, other = own_ref[...].astype(f32), other_ref[...].astype(f32)
    x = jnp.concatenate([own, other], axis=0)
    even = (x[:, :HALF] + x[:, HALF:]).astype(bf16)
    odd = (x[:, :HALF] - x[:, HALF:]).astype(bf16)
    parts = []
    for side, lo in ((even, 0), (odd, QUARTER), (even, NF), (odd, NF + QUARTER)):
        parts.append(jnp.dot(side, dft_ref[:, lo : lo + QUARTER], preferred_element_type=f32))
    power = sum(part * part for part in parts)
    bands = NF // BAND
    bin_band = lax.broadcasted_iota(jnp.int32, (QUARTER, bands), 0) // (BAND // 2)
    member = (bin_band == lax.broadcasted_iota(jnp.int32, (QUARTER, bands), 1)).astype(f32)
    bin_band_t = lax.broadcasted_iota(jnp.int32, (bands, QUARTER), 1) // (BAND // 2)
    member_t = (bin_band_t == lax.broadcasted_iota(jnp.int32, (bands, QUARTER), 0)).astype(f32)
    high = lax.Precision.HIGHEST
    band_power = jnp.dot(power, member, precision=high, preferred_element_type=f32)
    band_power = band_power / (2 * BAND) + 1e-05
    live = live_ref[...]
    scaling = jnp.concatenate([live, live], axis=0) / jnp.sqrt(band_power)
    scaling = jnp.dot(scaling, member_t, precision=high, preferred_element_type=f32)
    for i, part in enumerate(parts):
        out_ref[:, i * QUARTER : (i + 1) * QUARTER] = (part * scaling).astype(bf16)


def whiten(own, other, live, dft):
    rows = own.shape[0]
    return pl.pallas_call(
        whiten_kernel,
        out_shape=jax.ShapeDtypeStruct((2 * rows, 2 * NF), bf16),
        compiler_params=pltpu.CompilerParams(vmem_limit_bytes=VMEM_LIMIT),
        cost_estimate=pl.CostEstimate(
            flops=4 * rows * HALF * 2 * NF, bytes_accessed=4 * HALF * NF, transcendentals=0
        ),
        name="whiten",
    )(own, other, live, dft)


def select_kernel(places_ref, *refs):
    units, out_ref = refs[:-1], refs[-1]
    rows = units[0].shape[0]
    places = places_ref[...]
    total = jnp.zeros(out_ref.shape, f32)
    for u, unit in enumerate(units):
        ids = lax.broadcasted_iota(jnp.int32, (places.shape[0], rows), 1) + u * rows
        pick = (ids == places).astype(bf16)
        total = total + jnp.dot(pick, unit[...], preferred_element_type=f32)
    out_ref[...] = total.astype(bf16)


def select(places, units):
    return pl.pallas_call(
        select_kernel,
        out_shape=jax.ShapeDtypeStruct((places.shape[0], 2 * NF), bf16),
        compiler_params=pltpu.CompilerParams(vmem_limit_bytes=VMEM_LIMIT),
        name="select",
    )(places, *units)


def gather_kernel(rows_ref, src_ref, lag_ref, *refs):
    units, (out_ref, cross) = refs[:-2], refs[-2:]
    receivers = units[0].shape[0] // 2
    count = len(units)
    group = max(1, 256 // receivers)
    for first in range(0, count, group):
        members = list(range(first, min(count, first + group)))
        for lo in range(0, NF, 256):
            real = [
                jnp.broadcast_to(src_ref[0, s : s + 1, lo : lo + 256], (receivers, 256)).astype(bf16)
                for s in range(2)
            ]
            imag = [
                jnp.broadcast_to(
                    src_ref[0, s : s + 1, NF + lo : NF + lo + 256], (receivers, 256)
                ).astype(bf16)
                for s in range(2)
            ]
            for u in members:
                cr, ci = None, None
                for s in range(2):
                    wr = units[u][s * receivers : (s + 1) * receivers, lo : lo + 256]
                    wi = units[u][s * receivers : (s + 1) * receivers, NF + lo : NF + lo + 256]
                    r = real[s] * wr + imag[s] * wi
                    i = imag[s] * wr - real[s] * wi
                    cr = r if cr is None else cr + r
                    ci = i if ci is None else ci + i
                cross[u * receivers : (u + 1) * receivers, lo : lo + 256] = cr
                cross[u * receivers : (u + 1) * receivers, NF + lo : NF + lo + 256] = ci
        top, end = members[0] * receivers, (members[-1] + 1) * receivers
        stacked = jnp.dot(cross[top:end, :], lag_ref[...], preferred_element_type=f32)
        mean_sq = jnp.mean(stacked * stacked, axis=-1, keepdims=True)
        normed = (stacked / jnp.sqrt(mean_sq + 1e-06)).astype(bf16)
        for n, u in enumerate(members):
            out_ref[0, rows_ref[u]] = normed[n * receivers : (n + 1) * receivers, :]


def gather_slots(rows, src, lag, units):
    capacity = src.shape[0]
    count = len(units)
    receivers = units[0].shape[0] // 2
    whole = pl.BlockSpec(units[0].shape, lambda g, rows: (0, 0))
    return pl.pallas_call(
        gather_kernel,
        out_shape=jax.ShapeDtypeStruct((capacity, count, receivers, LAGS), bf16),
        grid_spec=pltpu.PrefetchScalarGridSpec(
            num_scalar_prefetch=1,
            grid=(capacity,),
            in_specs=[
                pl.BlockSpec((1, 2, 2 * NF), lambda g, rows: (g, 0, 0)),
                pl.BlockSpec(lag.shape, lambda g, rows: (0, 0)),
            ]
            + [whole] * count,
            out_specs=pl.BlockSpec((1, count, receivers, LAGS), lambda g, rows: (g, 0, 0, 0)),
            scratch_shapes=[pltpu.VMEM((count * receivers, 2 * NF), bf16)],
        ),
        compiler_params=pltpu.CompilerParams(vmem_limit_bytes=VMEM_LIMIT),
        name="gather_slots",
    )(rows, src, lag, *units)


def local_pairs(traces, live_mask, sources, owners):
    row_count = lax.axis_size("row")
    samples = traces[0]
    channels = samples.shape[0]
    num_sources = sources.shape[0]
    receivers = channels // 2
    me, side = lax.axis_index("row"), lax.axis_index("seg")
    swap = [(0, 1), (1, 0)]

    away = lax.dynamic_slice_in_dim(samples, (1 - side) * receivers, receivers, 0)
    other = lax.ppermute(away, "seg", swap)
    own = lax.dynamic_slice_in_dim(samples, side * receivers, receivers, 0)
    live = lax.dynamic_slice_in_dim(live_mask, side * receivers, receivers, 0)
    dft, lag = make_tables()
    unit = whiten(own, other, live.astype(f32)[:, None], dft)

    depth = row_count // 4

    def shifted(value, step):
        pairs = [(r, (r // 4 - step) % depth * 4 + r % 4) for r in range(row_count)]
        return lax.ppermute(value, "row", pairs)

    def flipped(value, bit):
        return lax.ppermute(value, "row", [(r, r ^ bit) for r in range(row_count)])

    steps = [0]
    for d in range(1, depth // 2 + 1):
        steps += [d] if 2 * d == depth else [d, depth - d]
    units = {}
    for d in steps:
        units[d, 0, 0] = shifted(unit, d) if d else unit
        units[d, 1, 0] = flipped(units[d, 0, 0], 2)
    for d in steps:
        for e in range(2):
            units[d, e, 1] = flipped(units[d, e, 0], 1)
    keys = [(d, e, k) for d in range(depth) for e in range(2) for k in range(2)]
    units = [units[key] for key in keys]
    rows = jnp.stack(
        [(me // 4 + d) % depth * 4 + (me % 4 ^ (2 * e + k)) for d, e, k in keys]
    ).astype(jnp.int32)

    capacity = 3 * num_sources // row_count
    owner_ids = owners[:, 0]
    order_ids = jnp.arange(num_sources, dtype=jnp.int32)
    earlier = (owner_ids[:, None] == owner_ids[None, :]) & (order_ids[None, :] < order_ids[:, None])
    slot_rank = jnp.sum(earlier.astype(jnp.int32), axis=1)
    mine = (owner_ids == me)[None, :] & (slot_rank[None, :] == jnp.arange(capacity)[:, None])
    channel = jnp.sum(jnp.where(mine, sources[None, :], 0), axis=1)
    block, within = channel // channels, channel % channels
    held = jnp.any(mine, axis=1) & (within // receivers == side)
    relative = (block // 4 - me // 4) % depth * 4 + ((block ^ me) % 4)
    place = relative * channels + within % receivers
    place = jnp.where(held, place, -1)
    place_other = jnp.where(held, place + receivers, -1)
    pad = -capacity % 16
    places = jnp.concatenate(
        [jnp.pad(p, (0, pad), constant_values=-1) for p in (place, place_other)]
    )[:, None]
    chosen = select(places, units)
    from_other = lax.ppermute(chosen, "seg", swap)
    padded = capacity + pad
    src = jnp.stack(
        [
            chosen[:capacity].astype(f32) + from_other[padded : padded + capacity].astype(f32),
            chosen[padded : padded + capacity].astype(f32) + from_other[:capacity].astype(f32),
        ],
        axis=1,
    )
    return gather_slots(rows, src, lag, units)


def solution(mesh):
    placed = (P(("run", "seg"), "row", "col"), P(("run", "row")), P(), P())
    shape = mesh.shape
    pairs = shape["col"] == 1 and shape["seg"] == 2 and shape["row"] % 4 == 0
    return jax.shard_map(
        local_pairs if pairs else local_general,
        mesh=mesh,
        in_specs=placed,
        out_specs=P(("run", "row"), None, ("col", "seg"), None),
        check_vma=False,
    )
```

```python
import functools
import math

import jax
import jax.numpy as jnp
from jax import lax
from jax.experimental import pallas as pl
from jax.experimental.pallas import tpu as pltpu
from jax.sharding import PartitionSpec as P


NT = 2048
NF = 1024
LAGS = 256
BAND = 64


two_pi = 2.0 * math.pi
f32 = jnp.float32
bf16 = jnp.bfloat16


def turn_table(first_ids, second_ids, period):
    product = first_ids[:, None] * second_ids[None, :] % period
    return product.astype(jnp.float32) * (two_pi / period)


def lag_matrix(bin_ids):
    lag_ids = jnp.arange(LAGS, dtype=jnp.int32) - LAGS // 2 + NT
    lag_angles = turn_table(bin_ids, lag_ids, NT)
    return jnp.concatenate(
        [jnp.cos(lag_angles).astype(jnp.bfloat16), -jnp.sin(lag_angles).astype(jnp.bfloat16)],
        axis=0,
    )


def correlate(recv_real, recv_imag, real_source, imag_source, lag_table):
    cross_real = (
        real_source[:, None, :] * recv_real[:, :, None]
        + imag_source[:, None, :] * recv_imag[:, :, None]
    ).astype(jnp.bfloat16)
    cross_imag = (
        imag_source[:, None, :] * recv_real[:, :, None]
        - real_source[:, None, :] * recv_imag[:, :, None]
    ).astype(jnp.bfloat16)
    stacked_cross = jnp.concatenate([cross_real, cross_imag], axis=0)
    return jnp.einsum("fl,fgv->gvl", lag_table, stacked_cross, preferred_element_type=jnp.float32)


def local_general(traces, live_mask, sources, owners):
    col_count = lax.axis_size("col")
    seg_count = lax.axis_size("seg")
    row_count = lax.axis_size("row")
    samples = traces[0]
    channels = samples.shape[0]
    local_width = samples.shape[1]
    num_sources = sources.shape[0]
    first_sample = lax.axis_index("col") * local_width
    half_bins = NF // col_count
    sample_ids = first_sample + jnp.arange(local_width, dtype=jnp.int32)
    bin_ids = jnp.arange(half_bins * lax.axis_size("col"), dtype=jnp.int32)
    angles = turn_table(sample_ids, bin_ids, NT)
    cosine = jnp.cos(angles).astype(jnp.bfloat16)
    sine_table = jnp.sin(angles).astype(jnp.bfloat16)
    real_part = jnp.einsum("tf,ct->fc", cosine, samples, preferred_element_type=jnp.float32)
    imag_part = -jnp.einsum("tf,ct->fc", sine_table, samples, preferred_element_type=jnp.float32)
    spectra = lax.psum_scatter(
        jnp.concatenate([real_part, imag_part], axis=1).astype(jnp.bfloat16),
        "col",
        scatter_dimension=0,
        tiled=True,
    ).astype(jnp.float32)
    squares = (spectra * spectra).reshape(half_bins // BAND, BAND, 2, channels)
    band_power = jnp.sum(squares, axis=(1, 2)) / (2 * BAND) + 1e-05
    scaling = live_mask.astype(jnp.float32)[None, :] / jnp.sqrt(band_power)
    scaling = jnp.repeat(scaling, BAND, axis=0)
    whitened = (
        (spectra.reshape(half_bins, 2, channels) * scaling[:, None, :])
        .reshape(half_bins, 2 * channels)
        .astype(jnp.bfloat16)
    )
    white_real = whitened[:, :channels]
    white_imag = whitened[:, channels:]
    everyone = lax.all_gather(whitened, "row", axis=1, tiled=True)
    block_ids = sources // channels
    within = sources % channels
    real_cols = block_ids * (2 * channels) + within
    source_real = jnp.take(everyone, real_cols, axis=1)
    source_imag = jnp.take(everyone, real_cols + channels, axis=1)
    receivers = channels // (col_count * seg_count)
    bin_ids = lax.axis_index("col") * half_bins + jnp.arange(half_bins, dtype=jnp.int32)
    lag_table = lag_matrix(bin_ids)
    real_source = source_real.astype(jnp.float32)
    imag_source = source_imag.astype(jnp.float32)

    def one_group(offset):
        recv_real = lax.dynamic_slice_in_dim(white_real, offset, receivers, 1).astype(jnp.float32)
        recv_imag = lax.dynamic_slice_in_dim(white_imag, offset, receivers, 1).astype(jnp.float32)
        return correlate(recv_real, recv_imag, real_source, imag_source, lag_table)

    offsets = (
        jnp.arange(receivers * lax.axis_size(("col", "seg")) // receivers, dtype=jnp.int32)
        * receivers
    )
    blocks = lax.map(one_group, offsets)
    stacked = lax.psum_scatter(
        blocks.reshape(receivers * lax.axis_size(("col", "seg")), num_sources, LAGS).astype(
            jnp.bfloat16
        ),
        ("col", "seg"),
        scatter_dimension=0,
        tiled=True,
    ).astype(jnp.float32)
    mean_sq = jnp.mean(stacked * stacked, axis=-1, keepdims=True)
    normed = (stacked * lax.rsqrt(mean_sq + 1e-06)).astype(jnp.bfloat16)
    capacity = 3 * num_sources // row_count
    owner_ids = owners[:, 0]
    order_ids = jnp.arange(num_sources, dtype=jnp.int32)
    earlier = (owner_ids[:, None] == owner_ids[None, :]) & (order_ids[None, :] < order_ids[:, None])
    slot_rank = jnp.sum(earlier.astype(jnp.int32), axis=1)
    slot_ids = owner_ids * capacity + slot_rank
    placing = (
        jnp.arange(row_count * capacity, dtype=jnp.int32)[:, None] == slot_ids[None, :]
    ).astype(jnp.bfloat16)
    outgoing = jnp.einsum(
        "sv,gvl->sgl", placing, normed, preferred_element_type=jnp.float32
    ).astype(jnp.bfloat16)
    return lax.all_to_all(outgoing[:, None], "row", split_axis=0, concat_axis=1, tiled=True)


HALF = NT // 2
QUARTER = NF // 2
VMEM_LIMIT = 16 * 1024 * 1024


def turn(steps):
    steps = steps % NT
    quarter = (steps + NT // 8) // (NT // 4)
    x = (steps - quarter * (NT // 4)).astype(f32) * (two_pi / NT)
    y = x * x
    c = 1.0 + y * (-1 / 2 + y * (1 / 24 + y * (-1 / 720 + y * (1 / 40320 - y / 3628800))))
    s = x * (1.0 + y * (-1 / 6 + y * (1 / 120 + y * (-1 / 5040 + y / 362880))))
    odd, back, low = quarter % 2 == 1, quarter % 4 >= 2, (quarter + 1) % 4 >= 2
    cos, sin = jnp.where(odd, s, c), jnp.where(odd, c, s)
    return jnp.where(low, -cos, cos), jnp.where(back, -sin, sin)


def rows_of(count, scale, first, others):
    ids = lax.broadcasted_iota(jnp.int32, (count, others.shape[1]), 0)
    return turn((ids * scale + first) * others)


def fill_dft(dft_ref, coarse_c, coarse_s, base_c, base_s):
    blocks = HALF // 64
    places = lax.broadcasted_iota(jnp.int32, (1, NF), 1)
    bins = jnp.where(places < QUARTER, 2 * places, 2 * places - NF + 1)
    coarse_c[...], coarse_s[...] = rows_of(blocks, 64, 0, bins)
    middle_c, middle_s = rows_of(8, 8, 0, bins)
    fine_c, fine_s = rows_of(8, 1, 0, bins)
    for b in range(8):
        cb, sb = middle_c[b : b + 1, :], middle_s[b : b + 1, :]
        base_c[8 * b : 8 * b + 8, :] = fine_c * cb - fine_s * sb
        base_s[8 * b : 8 * b + 8, :] = fine_s * cb + fine_c * sb
    for a in range(blocks):
        for lo in range(0, NF, 256):
            ca, sa = coarse_c[a : a + 1, lo : lo + 256], coarse_s[a : a + 1, lo : lo + 256]
            bc, bs = base_c[:, lo : lo + 256], base_s[:, lo : lo + 256]
            dft_ref[64 * a : 64 * a + 64, lo : lo + 256] = (bc * ca - bs * sa).astype(bf16)
            dft_ref[64 * a : 64 * a + 64, NF + lo : NF + lo + 256] = (-bs * ca - bc * sa).astype(bf16)


def dft_scratch():
    coarse, base = pltpu.VMEM((HALF // 64, NF), f32), pltpu.VMEM((64, NF), f32)
    return [coarse, coarse, base, base]


def tables_kernel(dft_ref, lag_ref, coarse_c, coarse_s, base_c, base_s):
    fill_dft(dft_ref, coarse_c, coarse_s, base_c, base_s)
    lags = lax.broadcasted_iota(jnp.int32, (1, LAGS), 1) - LAGS // 2 + NT
    groups = QUARTER // 64
    far_c, far_s = rows_of(groups, 128, 0, lags)
    middle_c, middle_s = rows_of(8, 16, 0, lags)
    for odd in range(2):
        fine_c, fine_s = rows_of(8, 2, odd, lags)
        for b in range(8):
            cb, sb = middle_c[b : b + 1, :], middle_s[b : b + 1, :]
            base_c[8 * b : 8 * b + 8, :LAGS] = fine_c * cb - fine_s * sb
            base_s[8 * b : 8 * b + 8, :LAGS] = fine_s * cb + fine_c * sb
        for a in range(groups):
            ca, sa = far_c[a : a + 1, :], far_s[a : a + 1, :]
            bc, bs = base_c[:, :LAGS], base_s[:, :LAGS]
            at = QUARTER * odd + 64 * a
            lag_ref[at : at + 64, :] = (bc * ca - bs * sa).astype(bf16)
            lag_ref[NF + at : NF + at + 64, :] = (-bs * ca - bc * sa).astype(bf16)


def make_tables():
    return pl.pallas_call(
        tables_kernel,
        out_shape=(
            jax.ShapeDtypeStruct((HALF, 2 * NF), bf16),
            jax.ShapeDtypeStruct((2 * NF, LAGS), bf16),
        ),
        scratch_shapes=dft_scratch(),
        compiler_params=pltpu.CompilerParams(vmem_limit_bytes=VMEM_LIMIT),
        cost_estimate=pl.CostEstimate(
            flops=6 * HALF * NF, bytes_accessed=4 * HALF * NF, transcendentals=0
        ),
        name="tables",
    )()


def whiten_rows(own, other, dft_ref, out_ref):
    x = jnp.concatenate([own, other], axis=0).astype(f32)
    even = (x[:, :HALF] + x[:, HALF:]).astype(bf16)
    odd = (x[:, :HALF] - x[:, HALF:]).astype(bf16)
    parts = []
    for side, lo in ((even, 0), (odd, QUARTER), (even, NF), (odd, NF + QUARTER)):
        parts.append(jnp.dot(side, dft_ref[:, lo : lo + QUARTER], preferred_element_type=f32))
    power = sum(part * part for part in parts)
    bands = NF // BAND
    bin_band = lax.broadcasted_iota(jnp.int32, (QUARTER, bands), 0) // (BAND // 2)
    member = (bin_band == lax.broadcasted_iota(jnp.int32, (QUARTER, bands), 1)).astype(f32)
    bin_band_t = lax.broadcasted_iota(jnp.int32, (bands, QUARTER), 1) // (BAND // 2)
    member_t = (bin_band_t == lax.broadcasted_iota(jnp.int32, (bands, QUARTER), 0)).astype(f32)
    high = lax.Precision.HIGHEST
    band_power = jnp.dot(power, member, precision=high, preferred_element_type=f32)
    scaling = lax.rsqrt(band_power / (2 * BAND) + 1e-05)
    scaling = jnp.dot(scaling, member_t, precision=high, preferred_element_type=f32)
    for i, part in enumerate(parts):
        white = (part * scaling).astype(bf16)
        out_ref[:, i * QUARTER : (i + 1) * QUARTER] = white.astype(out_ref.dtype)


def whiten_kernel(own_ref, other_ref, dft_ref, out_ref):
    whiten_rows(own_ref[...], other_ref[...], dft_ref, out_ref)


def whiten(own, other, dft):
    rows = own.shape[0]
    return pl.pallas_call(
        whiten_kernel,
        out_shape=jax.ShapeDtypeStruct((2 * rows, 2 * NF), bf16),
        compiler_params=pltpu.CompilerParams(vmem_limit_bytes=VMEM_LIMIT),
        cost_estimate=pl.CostEstimate(
            flops=4 * rows * HALF * 2 * NF, bytes_accessed=4 * HALF * NF, transcendentals=0
        ),
        name="whiten",
    )(own, other, dft)


def whiten_sources_kernel(own_ref, other_ref, out_ref, dft_ref, *scratch):
    fill_dft(dft_ref, *scratch)
    whiten_rows(own_ref[...], other_ref[...], dft_ref, out_ref)


def whiten_sources(own, other):
    rows = own.shape[0]
    return pl.pallas_call(
        whiten_sources_kernel,
        out_shape=jax.ShapeDtypeStruct((2 * rows, 2 * NF), f32),
        scratch_shapes=[pltpu.VMEM((HALF, 2 * NF), bf16)] + dft_scratch(),
        compiler_params=pltpu.CompilerParams(vmem_limit_bytes=VMEM_LIMIT),
        cost_estimate=pl.CostEstimate(
            flops=4 * rows * HALF * 2 * NF, bytes_accessed=4 * HALF * NF, transcendentals=0
        ),
        name="whiten_sources",
    )(own, other)


def front_kernel(at_ref, facts_ref, samples_ref, own_ref, away_ref, keep_ref, give_ref, held, picked):
    me, side, core, deep = at_ref[0], at_ref[1], at_ref[2], at_ref[3]
    channels = samples_ref.shape[0]
    receivers, half = own_ref.shape[0], keep_ref.shape[0]
    row_ids = lax.broadcasted_iota(jnp.int32, (channels, channels), 0)
    diagonal = row_ids == lax.broadcasted_iota(jnp.int32, (channels, channels), 1)
    mask = jnp.where(diagonal, facts_ref[0:1, :channels].astype(f32), 0.0).astype(bf16)
    held[...] = jnp.dot(mask, samples_ref[...], preferred_element_type=f32).astype(bf16)
    own_ref[...] = held[pl.ds(pl.multiple_of(side * receivers, receivers), receivers), :]
    away_ref[...] = held[pl.ds(pl.multiple_of((1 - side) * receivers, receivers), receivers), :]
    ids = lax.broadcasted_iota(jnp.int32, (channels, 2 * half), 0) + me * channels
    choose = (ids == facts_ref[1:2, : 2 * half]).astype(bf16)
    picked[...] = lax.dot_general(
        choose, held[...], (((0,), (0,)), ((), ())), preferred_element_type=f32
    ).astype(bf16)
    part = half // 2
    for out_ref, owner in ((keep_ref, core), (give_ref, 1 - core)):
        for n, side_y in enumerate((deep, 1 - deep)):
            first = pl.multiple_of(owner * half + side_y * part, part)
            out_ref[n * part : (n + 1) * part, :] = picked[pl.ds(first, part), :]


def front(at, live, sources, samples):
    channels, width = samples.shape
    count = sources.shape[0]
    longest = max(channels, count)
    facts = jnp.stack(
        [jnp.pad(live, (0, longest - channels)), jnp.pad(sources, (0, longest - count))]
    )
    shapes = [channels // 2, channels // 2, count // 2, count // 2]
    vmem = pl.BlockSpec(memory_space=pltpu.VMEM)
    return pl.pallas_call(
        front_kernel,
        out_shape=[jax.ShapeDtypeStruct((rows, width), bf16) for rows in shapes],
        in_specs=[pl.BlockSpec(memory_space=pltpu.SMEM), vmem, vmem],
        scratch_shapes=[pltpu.VMEM((channels, width), bf16), pltpu.VMEM((count, width), bf16)],
        compiler_params=pltpu.CompilerParams(vmem_limit_bytes=VMEM_LIMIT),
        cost_estimate=pl.CostEstimate(flops=1 << 24, bytes_accessed=1 << 20, transcendentals=0),
        name="front",
    )(at, facts, samples)


def gather_kernel(rows_ref, src_ref, lag_ref, *refs, count, per):
    units, out_ref = refs[:count], refs[-6]
    crosses, (stage, sem) = refs[-5:-2], refs[-2:]
    capacity = out_ref.shape[0]
    receivers = units[0].shape[0] // 2
    second = src_ref.shape[0] // 2
    width = 256
    copies = []
    starts = list(range(0, capacity, per))
    for g, first in enumerate(starts):
        slots = list(range(first, min(capacity, first + per)))
        cross = crosses[g % len(crosses)]
        for n, slot in enumerate(slots):
            for lo in range(0, NF, width):
                real0, imag0, real1, imag1 = [
                    jnp.broadcast_to(
                        src_ref[at : at + 1, first_bin : first_bin + width], (16, width)
                    ).astype(bf16)
                    for at in (slot, slot + second)
                    for first_bin in (lo, NF + lo)
                ]
                for u, unit in enumerate(units):
                    for top in range(0, receivers, 16):
                        wr0, wi0, wr1, wi1 = [
                            unit[at : at + 16, first_bin : first_bin + width]
                            for at in (top, receivers + top)
                            for first_bin in (lo, NF + lo)
                        ]
                        row = (n * count + u) * receivers + top
                        cross[row : row + 16, lo : lo + width] = (
                            real0 * wr0 + imag0 * wi0 + (real1 * wr1 + imag1 * wi1)
                        )
                        cross[row : row + 16, NF + lo : NF + lo + width] = (
                            imag0 * wr0 - real0 * wi0 + (imag1 * wr1 - real1 * wi1)
                        )
        filled = len(slots) * count * receivers
        stacked = jnp.dot(cross[:filled, :], lag_ref[...], preferred_element_type=f32)
        mean_sq = jnp.mean(stacked * stacked, axis=-1, keepdims=True)
        normed = (stacked * lax.rsqrt(mean_sq + 1e-06)).astype(bf16)
        normed = normed.reshape(len(slots), count, receivers, LAGS)
        for u in range(count):
            stage[u, first : first + len(slots)] = normed[:, u]
            copy = pltpu.make_async_copy(
                stage.at[u, pl.ds(first, len(slots))],
                out_ref.at[pl.ds(first, len(slots)), rows_ref[u]],
                sem.at[g * count + u],
            )
            copy.start()
            copies.append(copy)
    for copy in copies:
        copy.wait()


def gather_slots(rows, src, lag, units, held, capacity, row_count):
    count = len(units)
    receivers = units[0].shape[0] // 2
    per = 4
    steps = -(-capacity // per)
    vmem, anywhere = pl.BlockSpec(memory_space=pltpu.VMEM), pl.BlockSpec(memory_space=pl.ANY)
    prior = () if held is None else (held,)
    operands = (rows, src, lag, *units, *prior)
    return pl.pallas_call(
        functools.partial(gather_kernel, count=count, per=per),
        out_shape=jax.ShapeDtypeStruct((capacity, row_count, receivers, LAGS), bf16),
        in_specs=[pl.BlockSpec(memory_space=pltpu.SMEM)] + [vmem] * (2 + count) + [anywhere] * len(prior),
        out_specs=anywhere,
        input_output_aliases={len(operands) - 1: 0} if prior else {},
        scratch_shapes=[pltpu.VMEM((per * count * receivers, 2 * NF), bf16)] * 3
        + [
            pltpu.VMEM((count, capacity, receivers, LAGS), bf16),
            pltpu.SemaphoreType.DMA((steps * count,)),
        ],
        compiler_params=pltpu.CompilerParams(vmem_limit_bytes=VMEM_LIMIT),
        cost_estimate=pl.CostEstimate(
            flops=4 * NF * LAGS * capacity * count * receivers, bytes_accessed=4 << 20, transcendentals=0
        ),
        name="gather_slots",
    )(*operands)


def slots_kernel(mine_ref, sib_ref, found_ref, more_ref, own_ref, give_ref):
    part = found_ref.shape[0]
    for index_ref, out_ref in ((mine_ref, own_ref), (sib_ref, give_ref)):
        chosen = jnp.zeros(out_ref.shape, f32)
        ids = lax.broadcasted_iota(jnp.int32, (out_ref.shape[0], part), 1)
        for first, rows_ref in ((0, found_ref), (part, more_ref)):
            choose = (ids + first == index_ref[...]).astype(bf16)
            chosen += jnp.dot(choose, rows_ref[...], preferred_element_type=f32)
        out_ref[...] = chosen.astype(bf16)


def pick_slots(mine, sibling, found, more):
    half = jax.ShapeDtypeStruct((mine.shape[0], found.shape[1]), bf16)
    return pl.pallas_call(
        slots_kernel,
        out_shape=(half, half),
        compiler_params=pltpu.CompilerParams(vmem_limit_bytes=VMEM_LIMIT),
        cost_estimate=pl.CostEstimate(flops=1 << 23, bytes_accessed=1 << 19, transcendentals=0),
        name="pick_slots",
    )(mine[:, None], sibling[:, None], found, more)


def pairs_body(traces, live_mask, sources, owners):
    row_count = lax.axis_size("row")
    samples = traces[0]
    num_sources = sources.shape[0]
    me, side = lax.axis_index("row"), lax.axis_index("seg")
    swap = [(0, 1), (1, 0)]
    capacity = 3 * num_sources // row_count

    def flipped(value, bit):
        return lax.ppermute(value, "row", [(r, r ^ bit) for r in range(row_count)])

    half = num_sources // 2
    core = me % 2
    kept_first = core * half
    lane = me // 2 % 2
    at = jnp.stack([me, side, core, lane]).astype(jnp.int32)
    own, away, found, give = front(at, live_mask, sources, samples)
    other = lax.ppermute(away, "seg", swap)
    found = found + flipped(give, 1)
    part = half // 2
    found = found[:part] + flipped(found[part:], 2)
    for bit in (8, 4):
        found = found + flipped(found, bit)
    more = flipped(found, 2)

    owner_ids = owners[:, 0]
    order_ids = jnp.arange(num_sources, dtype=jnp.int32)
    earlier = (owner_ids[:, None] == owner_ids[None, :]) & (order_ids[None, :] < order_ids[:, None])
    slot_rank = jnp.sum(earlier.astype(jnp.int32), axis=1)
    padded = capacity + -capacity % 16

    def slot_places(row):
        slots = jnp.arange(padded, dtype=jnp.int32)
        taken = (owner_ids == row)[None, :] & (slot_rank[None, :] == slots[:, None])
        taken = taken & ((order_ids >= kept_first) & (order_ids < kept_first + half))[None, :]
        places = (order_ids - kept_first) ^ (lane * part)
        return jnp.max(jnp.where(taken, places[None, :], -1), axis=1)

    own_src, sib_src = pick_slots(slot_places(me), slot_places(me ^ 1), found, more)
    own_src = own_src + flipped(sib_src, 1)
    other_src = lax.ppermute(own_src, "seg", swap)

    dft, lag = make_tables()
    unit = whiten(own, other, dft)

    depth = row_count // 4
    chips = 2 * depth
    place = jnp.where(lane == 0, me // 4, chips - 1 - me // 4)

    def row_at(position):
        return jnp.where(position < depth, 4 * position, 4 * (chips - 1 - position) + 2)

    def chip_row(position):
        return 4 * position if position < depth else 4 * (chips - 1 - position) + 2

    held = {0: unit}
    for k in range(1, depth + 1):
        for sign in (1, -1):
            if 2 * k == chips and sign < 0:
                continue
            moves = [
                (chip_row(p) + c, chip_row((p + sign) % chips) + c) for p in range(chips) for c in (0, 1)
            ]
            held[-sign * k] = lax.ppermute(held[-sign * (k - 1)], "row", moves)
    order = [0]
    for k in range(1, depth + 1):
        order += [-k, k]
    order = order[:-1]
    pairs = {}
    for d in order:
        pairs[d] = (held[d], flipped(held[d], 1))
    src = whiten_sources(own_src, other_src)
    out = None
    for n in range(depth):
        places = order[2 * n : 2 * n + 2]
        rows = jnp.stack(
            [row_at((place + d) % chips) + other for d in places for other in (core, 1 - core)]
        ).astype(jnp.int32)
        group = [value for d in places for value in pairs[d]]
        out = gather_slots(rows, src, lag, group, out, capacity, row_count)
    return out


def local_pairs(traces, live_mask, sources, owners):
    return pairs_body(traces, live_mask, sources, owners)


def solution(mesh):
    placed = (P(("run", "seg"), "row", "col"), P(("run", "row")), P(), P())
    shape = mesh.shape
    pairs = shape["col"] == 1 and shape["seg"] == 2 and shape["row"] == 16
    return jax.shard_map(
        local_pairs if pairs else local_general,
        mesh=mesh,
        in_specs=placed,
        out_specs=P(("run", "row"), None, ("col", "seg"), None),
        check_vma=False,
    )
```

```python
import functools
import math

import jax
import jax.numpy as jnp
from jax import lax
from jax.experimental import pallas as pl
from jax.experimental.pallas import tpu as pltpu
from jax.sharding import PartitionSpec as P


NT = 2048
NF = 1024
LAGS = 256
BAND = 64


two_pi = 2.0 * math.pi
f32 = jnp.float32
bf16 = jnp.bfloat16


def turn_table(first_ids, second_ids, period):
    product = first_ids[:, None] * second_ids[None, :] % period
    return product.astype(jnp.float32) * (two_pi / period)


def lag_matrix(bin_ids):
    lag_ids = jnp.arange(LAGS, dtype=jnp.int32) - LAGS // 2 + NT
    lag_angles = turn_table(bin_ids, lag_ids, NT)
    return jnp.concatenate(
        [jnp.cos(lag_angles).astype(jnp.bfloat16), -jnp.sin(lag_angles).astype(jnp.bfloat16)],
        axis=0,
    )


def correlate(recv_real, recv_imag, real_source, imag_source, lag_table):
    cross_real = (
        real_source[:, None, :] * recv_real[:, :, None]
        + imag_source[:, None, :] * recv_imag[:, :, None]
    ).astype(jnp.bfloat16)
    cross_imag = (
        imag_source[:, None, :] * recv_real[:, :, None]
        - real_source[:, None, :] * recv_imag[:, :, None]
    ).astype(jnp.bfloat16)
    stacked_cross = jnp.concatenate([cross_real, cross_imag], axis=0)
    return jnp.einsum("fl,fgv->gvl", lag_table, stacked_cross, preferred_element_type=jnp.float32)


def local_general(traces, live_mask, sources, owners):
    col_count = lax.axis_size("col")
    seg_count = lax.axis_size("seg")
    row_count = lax.axis_size("row")
    samples = traces[0]
    channels = samples.shape[0]
    local_width = samples.shape[1]
    num_sources = sources.shape[0]
    first_sample = lax.axis_index("col") * local_width
    half_bins = NF // col_count
    sample_ids = first_sample + jnp.arange(local_width, dtype=jnp.int32)
    bin_ids = jnp.arange(half_bins * lax.axis_size("col"), dtype=jnp.int32)
    angles = turn_table(sample_ids, bin_ids, NT)
    cosine = jnp.cos(angles).astype(jnp.bfloat16)
    sine_table = jnp.sin(angles).astype(jnp.bfloat16)
    real_part = jnp.einsum("tf,ct->fc", cosine, samples, preferred_element_type=jnp.float32)
    imag_part = -jnp.einsum("tf,ct->fc", sine_table, samples, preferred_element_type=jnp.float32)
    spectra = lax.psum_scatter(
        jnp.concatenate([real_part, imag_part], axis=1).astype(jnp.bfloat16),
        "col",
        scatter_dimension=0,
        tiled=True,
    ).astype(jnp.float32)
    squares = (spectra * spectra).reshape(half_bins // BAND, BAND, 2, channels)
    band_power = jnp.sum(squares, axis=(1, 2)) / (2 * BAND) + 1e-05
    scaling = live_mask.astype(jnp.float32)[None, :] / jnp.sqrt(band_power)
    scaling = jnp.repeat(scaling, BAND, axis=0)
    whitened = (
        (spectra.reshape(half_bins, 2, channels) * scaling[:, None, :])
        .reshape(half_bins, 2 * channels)
        .astype(jnp.bfloat16)
    )
    white_real = whitened[:, :channels]
    white_imag = whitened[:, channels:]
    everyone = lax.all_gather(whitened, "row", axis=1, tiled=True)
    block_ids = sources // channels
    within = sources % channels
    real_cols = block_ids * (2 * channels) + within
    source_real = jnp.take(everyone, real_cols, axis=1)
    source_imag = jnp.take(everyone, real_cols + channels, axis=1)
    receivers = channels // (col_count * seg_count)
    bin_ids = lax.axis_index("col") * half_bins + jnp.arange(half_bins, dtype=jnp.int32)
    lag_table = lag_matrix(bin_ids)
    real_source = source_real.astype(jnp.float32)
    imag_source = source_imag.astype(jnp.float32)

    def one_group(offset):
        recv_real = lax.dynamic_slice_in_dim(white_real, offset, receivers, 1).astype(jnp.float32)
        recv_imag = lax.dynamic_slice_in_dim(white_imag, offset, receivers, 1).astype(jnp.float32)
        return correlate(recv_real, recv_imag, real_source, imag_source, lag_table)

    offsets = (
        jnp.arange(receivers * lax.axis_size(("col", "seg")) // receivers, dtype=jnp.int32)
        * receivers
    )
    blocks = lax.map(one_group, offsets)
    stacked = lax.psum_scatter(
        blocks.reshape(receivers * lax.axis_size(("col", "seg")), num_sources, LAGS).astype(
            jnp.bfloat16
        ),
        ("col", "seg"),
        scatter_dimension=0,
        tiled=True,
    ).astype(jnp.float32)
    mean_sq = jnp.mean(stacked * stacked, axis=-1, keepdims=True)
    normed = (stacked * lax.rsqrt(mean_sq + 1e-06)).astype(jnp.bfloat16)
    capacity = 3 * num_sources // row_count
    owner_ids = owners[:, 0]
    order_ids = jnp.arange(num_sources, dtype=jnp.int32)
    earlier = (owner_ids[:, None] == owner_ids[None, :]) & (order_ids[None, :] < order_ids[:, None])
    slot_rank = jnp.sum(earlier.astype(jnp.int32), axis=1)
    slot_ids = owner_ids * capacity + slot_rank
    placing = (
        jnp.arange(row_count * capacity, dtype=jnp.int32)[:, None] == slot_ids[None, :]
    ).astype(jnp.bfloat16)
    outgoing = jnp.einsum(
        "sv,gvl->sgl", placing, normed, preferred_element_type=jnp.float32
    ).astype(jnp.bfloat16)
    return lax.all_to_all(outgoing[:, None], "row", split_axis=0, concat_axis=1, tiled=True)


HALF = NT // 2
QUARTER = NF // 2
VMEM_LIMIT = 16 * 1024 * 1024


def turn(steps):
    steps = steps % NT
    quarter = (steps + NT // 8) // (NT // 4)
    x = (steps - quarter * (NT // 4)).astype(f32) * (two_pi / NT)
    y = x * x
    c = 1.0 + y * (-1 / 2 + y * (1 / 24 + y * (-1 / 720 + y * (1 / 40320 - y / 3628800))))
    s = x * (1.0 + y * (-1 / 6 + y * (1 / 120 + y * (-1 / 5040 + y / 362880))))
    odd, back, low = quarter % 2 == 1, quarter % 4 >= 2, (quarter + 1) % 4 >= 2
    cos, sin = jnp.where(odd, s, c), jnp.where(odd, c, s)
    return jnp.where(low, -cos, cos), jnp.where(back, -sin, sin)


def rows_of(count, scale, first, others):
    ids = lax.broadcasted_iota(jnp.int32, (count, others.shape[1]), 0)
    return turn((ids * scale + first) * others)


def fill_dft(dft_ref, coarse_c, coarse_s, base_c, base_s):
    blocks = HALF // 64
    places = lax.broadcasted_iota(jnp.int32, (1, NF), 1)
    bins = jnp.where(places < QUARTER, 2 * places, 2 * places - NF + 1)
    coarse_c[...], coarse_s[...] = rows_of(blocks, 64, 0, bins)
    middle_c, middle_s = rows_of(8, 8, 0, bins)
    fine_c, fine_s = rows_of(8, 1, 0, bins)
    for b in range(8):
        cb, sb = middle_c[b : b + 1, :], middle_s[b : b + 1, :]
        base_c[8 * b : 8 * b + 8, :] = fine_c * cb - fine_s * sb
        base_s[8 * b : 8 * b + 8, :] = fine_s * cb + fine_c * sb
    for a in range(blocks):
        for lo in range(0, NF, 256):
            ca, sa = coarse_c[a : a + 1, lo : lo + 256], coarse_s[a : a + 1, lo : lo + 256]
            bc, bs = base_c[:, lo : lo + 256], base_s[:, lo : lo + 256]
            dft_ref[64 * a : 64 * a + 64, lo : lo + 256] = (bc * ca - bs * sa).astype(bf16)
            dft_ref[64 * a : 64 * a + 64, NF + lo : NF + lo + 256] = (-bs * ca - bc * sa).astype(bf16)


def dft_scratch():
    coarse, base = pltpu.VMEM((HALF // 64, NF), f32), pltpu.VMEM((64, NF), f32)
    return [coarse, coarse, base, base]


def tables_kernel(dft_ref, lag_ref, coarse_c, coarse_s, base_c, base_s):
    fill_dft(dft_ref, coarse_c, coarse_s, base_c, base_s)
    lags = lax.broadcasted_iota(jnp.int32, (1, LAGS), 1) - LAGS // 2 + NT
    groups = QUARTER // 64
    far_c, far_s = rows_of(groups, 128, 0, lags)
    middle_c, middle_s = rows_of(8, 16, 0, lags)
    for odd in range(2):
        fine_c, fine_s = rows_of(8, 2, odd, lags)
        for b in range(8):
            cb, sb = middle_c[b : b + 1, :], middle_s[b : b + 1, :]
            base_c[8 * b : 8 * b + 8, :LAGS] = fine_c * cb - fine_s * sb
            base_s[8 * b : 8 * b + 8, :LAGS] = fine_s * cb + fine_c * sb
        for a in range(groups):
            ca, sa = far_c[a : a + 1, :], far_s[a : a + 1, :]
            bc, bs = base_c[:, :LAGS], base_s[:, :LAGS]
            at = QUARTER * odd + 64 * a
            lag_ref[at : at + 64, :] = (bc * ca - bs * sa).astype(bf16)
            lag_ref[NF + at : NF + at + 64, :] = (-bs * ca - bc * sa).astype(bf16)


def make_tables():
    return pl.pallas_call(
        tables_kernel,
        out_shape=(
            jax.ShapeDtypeStruct((HALF, 2 * NF), bf16),
            jax.ShapeDtypeStruct((2 * NF, LAGS), bf16),
        ),
        scratch_shapes=dft_scratch(),
        compiler_params=pltpu.CompilerParams(vmem_limit_bytes=VMEM_LIMIT),
        cost_estimate=pl.CostEstimate(
            flops=6 * HALF * NF, bytes_accessed=4 * HALF * NF, transcendentals=0
        ),
        name="tables",
    )()


def whiten_rows(own, other, dft_ref, out_ref):
    x = jnp.concatenate([own, other], axis=0).astype(f32)
    even = (x[:, :HALF] + x[:, HALF:]).astype(bf16)
    odd = (x[:, :HALF] - x[:, HALF:]).astype(bf16)
    parts = []
    for side, lo in ((even, 0), (odd, QUARTER), (even, NF), (odd, NF + QUARTER)):
        parts.append(jnp.dot(side, dft_ref[:, lo : lo + QUARTER], preferred_element_type=f32))
    power = sum(part * part for part in parts)
    bands = NF // BAND
    bin_band = lax.broadcasted_iota(jnp.int32, (QUARTER, bands), 0) // (BAND // 2)
    member = (bin_band == lax.broadcasted_iota(jnp.int32, (QUARTER, bands), 1)).astype(f32)
    bin_band_t = lax.broadcasted_iota(jnp.int32, (bands, QUARTER), 1) // (BAND // 2)
    member_t = (bin_band_t == lax.broadcasted_iota(jnp.int32, (bands, QUARTER), 0)).astype(f32)
    high = lax.Precision.HIGHEST
    band_power = jnp.dot(power, member, precision=high, preferred_element_type=f32)
    scaling = lax.rsqrt(band_power / (2 * BAND) + 1e-05)
    scaling = jnp.dot(scaling, member_t, precision=high, preferred_element_type=f32)
    for i, part in enumerate(parts):
        white = (part * scaling).astype(bf16)
        out_ref[:, i * QUARTER : (i + 1) * QUARTER] = white.astype(out_ref.dtype)


def whiten_kernel(own_ref, other_ref, dft_ref, out_ref):
    whiten_rows(own_ref[...], other_ref[...], dft_ref, out_ref)


def whiten(own, other, dft):
    rows = own.shape[0]
    return pl.pallas_call(
        whiten_kernel,
        out_shape=jax.ShapeDtypeStruct((2 * rows, 2 * NF), bf16),
        compiler_params=pltpu.CompilerParams(vmem_limit_bytes=VMEM_LIMIT),
        cost_estimate=pl.CostEstimate(
            flops=4 * rows * HALF * 2 * NF, bytes_accessed=4 * HALF * NF, transcendentals=0
        ),
        name="whiten",
    )(own, other, dft)


def whiten_sources_kernel(own_ref, other_ref, out_ref, dft_ref, *scratch):
    fill_dft(dft_ref, *scratch)
    whiten_rows(own_ref[...], other_ref[...], dft_ref, out_ref)


def whiten_sources(own, other):
    rows = own.shape[0]
    return pl.pallas_call(
        whiten_sources_kernel,
        out_shape=jax.ShapeDtypeStruct((2 * rows, 2 * NF), f32),
        scratch_shapes=[pltpu.VMEM((HALF, 2 * NF), bf16)] + dft_scratch(),
        compiler_params=pltpu.CompilerParams(vmem_limit_bytes=VMEM_LIMIT),
        cost_estimate=pl.CostEstimate(
            flops=4 * rows * HALF * 2 * NF, bytes_accessed=4 * HALF * NF, transcendentals=0
        ),
        name="whiten_sources",
    )(own, other)


def front_kernel(at_ref, facts_ref, samples_ref, own_ref, away_ref, keep_ref, give_ref, held, picked):
    me, side, core, deep = at_ref[0], at_ref[1], at_ref[2], at_ref[3]
    channels = samples_ref.shape[0]
    receivers, half = own_ref.shape[0], keep_ref.shape[0]
    row_ids = lax.broadcasted_iota(jnp.int32, (channels, channels), 0)
    diagonal = row_ids == lax.broadcasted_iota(jnp.int32, (channels, channels), 1)
    mask = jnp.where(diagonal, facts_ref[0:1, :channels].astype(f32), 0.0).astype(bf16)
    held[...] = jnp.dot(mask, samples_ref[...], preferred_element_type=f32).astype(bf16)
    own_ref[...] = held[pl.ds(pl.multiple_of(side * receivers, receivers), receivers), :]
    away_ref[...] = held[pl.ds(pl.multiple_of((1 - side) * receivers, receivers), receivers), :]
    ids = lax.broadcasted_iota(jnp.int32, (channels, 2 * half), 0) + me * channels
    choose = (ids == facts_ref[1:2, : 2 * half]).astype(bf16)
    picked[...] = lax.dot_general(
        choose, held[...], (((0,), (0,)), ((), ())), preferred_element_type=f32
    ).astype(bf16)
    part = half // 2
    for out_ref, owner in ((keep_ref, core), (give_ref, 1 - core)):
        for n, side_y in enumerate((deep, 1 - deep)):
            first = pl.multiple_of(owner * half + side_y * part, part)
            out_ref[n * part : (n + 1) * part, :] = picked[pl.ds(first, part), :]


def front(at, live, sources, samples):
    channels, width = samples.shape
    count = sources.shape[0]
    longest = max(channels, count)
    facts = jnp.stack(
        [jnp.pad(live, (0, longest - channels)), jnp.pad(sources, (0, longest - count))]
    )
    shapes = [channels // 2, channels // 2, count // 2, count // 2]
    vmem = pl.BlockSpec(memory_space=pltpu.VMEM)
    return pl.pallas_call(
        front_kernel,
        out_shape=[jax.ShapeDtypeStruct((rows, width), bf16) for rows in shapes],
        in_specs=[pl.BlockSpec(memory_space=pltpu.SMEM), vmem, vmem],
        scratch_shapes=[pltpu.VMEM((channels, width), bf16), pltpu.VMEM((count, width), bf16)],
        compiler_params=pltpu.CompilerParams(vmem_limit_bytes=VMEM_LIMIT),
        cost_estimate=pl.CostEstimate(flops=1 << 24, bytes_accessed=1 << 20, transcendentals=0),
        name="front",
    )(at, facts, samples)


def gather_kernel(rows_ref, src_ref, lag_ref, *refs, count, per):
    units, out_ref = refs[:count], refs[-6]
    crosses, (stage, sem) = refs[-5:-2], refs[-2:]
    capacity = out_ref.shape[0]
    receivers = units[0].shape[0] // 2
    second = src_ref.shape[0] // 2
    width = 256
    copies = []
    starts = list(range(0, capacity, per))
    for g, first in enumerate(starts):
        slots = list(range(first, min(capacity, first + per)))
        cross = crosses[g % len(crosses)]
        for pair in range(0, len(slots), 2):
            members = slots[pair : pair + 2]
            for lo in range(0, NF, width):
                turned = [
                    jnp.broadcast_to(
                        src_ref[at : at + 1, first_bin : first_bin + width], (16, width)
                    ).astype(bf16)
                    for slot in members
                    for at in (slot, slot + second)
                    for first_bin in (lo, NF + lo)
                ]
                for u, unit in enumerate(units):
                    for top in range(0, receivers, 16):
                        wr0, wi0, wr1, wi1 = [
                            unit[at : at + 16, first_bin : first_bin + width]
                            for at in (top, receivers + top)
                            for first_bin in (lo, NF + lo)
                        ]
                        for m in range(len(members)):
                            real0, imag0, real1, imag1 = turned[4 * m : 4 * m + 4]
                            row = ((pair + m) * count + u) * receivers + top
                            cross[row : row + 16, lo : lo + width] = (
                                real0 * wr0 + imag0 * wi0 + (real1 * wr1 + imag1 * wi1)
                            )
                            cross[row : row + 16, NF + lo : NF + lo + width] = (
                                imag0 * wr0 - real0 * wi0 + (imag1 * wr1 - real1 * wi1)
                            )
        filled = len(slots) * count * receivers
        stacked = jnp.dot(cross[:filled, :], lag_ref[...], preferred_element_type=f32)
        mean_sq = jnp.mean(stacked * stacked, axis=-1, keepdims=True)
        normed = (stacked * lax.rsqrt(mean_sq + 1e-06)).astype(bf16)
        normed = normed.reshape(len(slots), count, receivers, LAGS)
        for u in range(count):
            stage[u, first : first + len(slots)] = normed[:, u]
            copy = pltpu.make_async_copy(
                stage.at[u, pl.ds(first, len(slots))],
                out_ref.at[pl.ds(first, len(slots)), rows_ref[u]],
                sem.at[g * count + u],
            )
            copy.start()
            copies.append(copy)
    for copy in copies:
        copy.wait()


def gather_slots(rows, src, lag, units, held, capacity, row_count):
    count = len(units)
    receivers = units[0].shape[0] // 2
    per = max(2, 16 // count)
    steps = -(-capacity // per)
    vmem, anywhere = pl.BlockSpec(memory_space=pltpu.VMEM), pl.BlockSpec(memory_space=pl.ANY)
    prior = () if held is None else (held,)
    operands = (rows, src, lag, *units, *prior)
    return pl.pallas_call(
        functools.partial(gather_kernel, count=count, per=per),
        out_shape=jax.ShapeDtypeStruct((capacity, row_count, receivers, LAGS), bf16),
        in_specs=[pl.BlockSpec(memory_space=pltpu.SMEM)] + [vmem] * (2 + count) + [anywhere] * len(prior),
        out_specs=anywhere,
        input_output_aliases={len(operands) - 1: 0} if prior else {},
        scratch_shapes=[pltpu.VMEM((per * count * receivers, 2 * NF), bf16)] * 3
        + [
            pltpu.VMEM((count, capacity, receivers, LAGS), bf16),
            pltpu.SemaphoreType.DMA((steps * count,)),
        ],
        compiler_params=pltpu.CompilerParams(vmem_limit_bytes=VMEM_LIMIT),
        cost_estimate=pl.CostEstimate(
            flops=4 * NF * LAGS * capacity * count * receivers, bytes_accessed=4 << 20, transcendentals=0
        ),
        name="gather_slots",
    )(*operands)


def slots_kernel(mine_ref, sib_ref, found_ref, more_ref, own_ref, give_ref):
    part = found_ref.shape[0]
    for index_ref, out_ref in ((mine_ref, own_ref), (sib_ref, give_ref)):
        chosen = jnp.zeros(out_ref.shape, f32)
        ids = lax.broadcasted_iota(jnp.int32, (out_ref.shape[0], part), 1)
        for first, rows_ref in ((0, found_ref), (part, more_ref)):
            choose = (ids + first == index_ref[...]).astype(bf16)
            chosen += jnp.dot(choose, rows_ref[...], preferred_element_type=f32)
        out_ref[...] = chosen.astype(bf16)


def pick_slots(mine, sibling, found, more):
    half = jax.ShapeDtypeStruct((mine.shape[0], found.shape[1]), bf16)
    return pl.pallas_call(
        slots_kernel,
        out_shape=(half, half),
        compiler_params=pltpu.CompilerParams(vmem_limit_bytes=VMEM_LIMIT),
        cost_estimate=pl.CostEstimate(flops=1 << 23, bytes_accessed=1 << 19, transcendentals=0),
        name="pick_slots",
    )(mine[:, None], sibling[:, None], found, more)


def pairs_body(traces, live_mask, sources, owners):
    row_count = lax.axis_size("row")
    samples = traces[0]
    num_sources = sources.shape[0]
    me, side = lax.axis_index("row"), lax.axis_index("seg")
    swap = [(0, 1), (1, 0)]
    capacity = 3 * num_sources // row_count

    def flipped(value, bit):
        return lax.ppermute(value, "row", [(r, r ^ bit) for r in range(row_count)])

    half = num_sources // 2
    core = me % 2
    kept_first = core * half
    lane = me // 2 % 2
    at = jnp.stack([me, side, core, lane]).astype(jnp.int32)
    own, away, found, give = front(at, live_mask, sources, samples)
    other = lax.ppermute(away, "seg", swap)
    found = found + flipped(give, 1)
    part = half // 2
    found = found[:part] + flipped(found[part:], 2)
    for bit in (8, 4):
        found = found + flipped(found, bit)
    more = flipped(found, 2)

    owner_ids = owners[:, 0]
    order_ids = jnp.arange(num_sources, dtype=jnp.int32)
    earlier = (owner_ids[:, None] == owner_ids[None, :]) & (order_ids[None, :] < order_ids[:, None])
    slot_rank = jnp.sum(earlier.astype(jnp.int32), axis=1)
    padded = capacity + -capacity % 16

    def slot_places(row):
        slots = jnp.arange(padded, dtype=jnp.int32)
        taken = (owner_ids == row)[None, :] & (slot_rank[None, :] == slots[:, None])
        taken = taken & ((order_ids >= kept_first) & (order_ids < kept_first + half))[None, :]
        places = (order_ids - kept_first) ^ (lane * part)
        return jnp.max(jnp.where(taken, places[None, :], -1), axis=1)

    own_src, sib_src = pick_slots(slot_places(me), slot_places(me ^ 1), found, more)
    own_src = own_src + flipped(sib_src, 1)
    other_src = lax.ppermute(own_src, "seg", swap)

    dft, lag = make_tables()
    unit = whiten(own, other, dft)

    depth = row_count // 4
    chips = 2 * depth
    place = jnp.where(lane == 0, me // 4, chips - 1 - me // 4)

    def row_at(position):
        return jnp.where(position < depth, 4 * position, 4 * (chips - 1 - position) + 2)

    def chip_row(position):
        return 4 * position if position < depth else 4 * (chips - 1 - position) + 2

    held = {0: unit}
    for k in range(1, depth + 1):
        for sign in (1, -1):
            if 2 * k == chips and sign < 0:
                continue
            moves = [
                (chip_row(p) + c, chip_row((p + sign) % chips) + c) for p in range(chips) for c in (0, 1)
            ]
            held[-sign * k] = lax.ppermute(held[-sign * (k - 1)], "row", moves)
    order = [0]
    for k in range(1, depth + 1):
        order += [-k, k]
    order = order[:-1]
    pairs = {}
    for d in order:
        pairs[d] = (held[d], flipped(held[d], 1))
    src = whiten_sources(own_src, other_src)
    out = None
    cuts = list(range(0, 2 * depth + 1, 2))
    for begin, end in zip(cuts, cuts[1:]):
        places = order[begin:end]
        rows = jnp.stack(
            [row_at((place + d) % chips) + other for d in places for other in (core, 1 - core)]
        ).astype(jnp.int32)
        group = [value for d in places for value in pairs[d]]
        out = gather_slots(rows, src, lag, group, out, capacity, row_count)
    return out


def local_pairs(traces, live_mask, sources, owners):
    return pairs_body(traces, live_mask, sources, owners)


def solution(mesh):
    placed = (P(("run", "seg"), "row", "col"), P(("run", "row")), P(), P())
    shape = mesh.shape
    pairs = shape["col"] == 1 and shape["seg"] == 2 and shape["row"] == 16
    return jax.shard_map(
        local_pairs if pairs else local_general,
        mesh=mesh,
        in_specs=placed,
        out_specs=P(("run", "row"), None, ("col", "seg"), None),
        check_vma=False,
    )
```
